512 devices in a mesh: seq: 32 (over z, core), feat: 16 (over y, x).
Axes of the slice: x: 4, y: 4, z: 16, core: 2. Of those that a mesh axis runs over, the one named last changes fastest.
Arguments:
- activations: bfloat16 [8192, 6144], P('seq', 'feat'), may hold values from -15 to 15
- ridge_scale: float32 [], replicated, may hold values from 0.5 to 2
Outputs:
- whitened: bfloat16 [8192, 6144], P('seq', 'feat')
The draws below stay inside these ranges and needn't reach their ends.
All inputs are finite; a program needn't handle non-finite values.
Results may differ from the reference program's by a relative error of at most 0.0033.
Values sent between devices are 32-bit elements; how exact they have to be, the bound alone decides.
No kernel may reach another device: no remote copies, remote signals or barrier semaphores. Data moves between devices by JAX's collectives and lax.ppermute only.
A program may use at most 128 MiB of HBM per device.

```python
import math
import jax
import jax.numpy as jnp
from jax import lax

D = 6144
RANK = 128
TOK_DEV = 256
ITERS = 1
ROOT_STEPS = 12
LEVELS = 5
TOKENS = 8192
N_SEQ = 32


def draw_activations(key, part):
    columns = jnp.exp(jax.random.uniform(jax.random.fold_in(key, 11), (D,), jnp.float32, math.log(0.3), math.log(3.0)))
    noise_rows = jnp.clip(jax.random.normal(jax.random.fold_in(key, 12), (TOKENS, D), jnp.float32), -5.0, 5.0)
    return (noise_rows * columns[None, :]).astype(jnp.bfloat16)


def setup_inputs(seed: int = 0) -> dict:
    streams_of = jax.random.split(jax.random.key(seed), 3)
    activations = draw_activations(jax.random.fold_in(streams_of[2], 71), 0)
    ridge_scale = jnp.clip(jnp.exp(jax.random.uniform(streams_of[1], (), jnp.float32, math.log(0.5), math.log(2.0))), 0.5, 2.0)
    return dict(activations=activations, ridge_scale=ridge_scale)


precise = lax.Precision.HIGHEST

def product(left_matrix, right_matrix):
    return jnp.dot(left_matrix, right_matrix, precision=precise)

def reduce_gram(stacked_gram):
    rank_size = stacked_gram.shape[0] // 2
    identity = jnp.eye(rank_size, dtype=stacked_gram.dtype)
    subspace = jnp.concatenate([identity, identity], axis=0) * 0.7071067811865476
    for repeat in range(ITERS):
        image_cols = product(stacked_gram, subspace)
        factor = jnp.linalg.cholesky(product(image_cols.T, image_cols))
        subspace = jax.scipy.linalg.solve_triangular(factor, image_cols.T, lower=True).T
    quotient = product(subspace.T, product(stacked_gram, subspace))
    quotient = 0.5 * (quotient + quotient.T)
    tail_mass = (jnp.trace(stacked_gram) - jnp.trace(quotient)) / rank_size
    root_factor = jnp.linalg.cholesky(quotient)
    inner_gram = product(root_factor.T, root_factor) + tail_mass * identity
    lower_factor = jnp.linalg.cholesky(inner_gram)
    return jax.scipy.linalg.solve_triangular(lower_factor, product(root_factor.T, subspace.T), lower=True)

def combine(earlier, later):
    own_gram = product(earlier, earlier.T)
    cross_gram = product(earlier, later.T)
    last_gram = product(later, later.T)
    stacked_gram = jnp.concatenate([jnp.concatenate([own_gram, cross_gram], 1), jnp.concatenate([cross_gram.T, last_gram], 1)], 0)
    mixing = reduce_gram(stacked_gram)
    return product(mixing, jnp.concatenate([earlier, later], 0))

def square_root(matrix):
    identity = jnp.eye(matrix.shape[0], dtype=matrix.dtype)
    norm_size = jnp.sqrt(jnp.sum(matrix * matrix))
    current = matrix / norm_size
    partner = identity
    for repeat in range(ROOT_STEPS):
        middle = 1.5 * identity - 0.5 * product(partner, current)
        current = product(current, middle)
        partner = product(middle, partner)
    return current * jnp.sqrt(norm_size)

def whiten(slab_rows, prefix, seen_rows, ridge_scale):
    scaled = prefix * lax.rsqrt(seen_rows * ridge_scale)
    small_gram = product(scaled, scaled.T)
    identity = jnp.eye(small_gram.shape[0], dtype=small_gram.dtype)
    shifted = identity + small_gram
    total_gram = shifted + square_root(shifted)
    total_gram = 0.5 * (total_gram + total_gram.T)
    half_basis = scaled.astype(jnp.bfloat16)
    projection = jnp.dot(slab_rows.astype(jnp.float32), half_basis.T.astype(jnp.float32), preferred_element_type=jnp.float32)
    coefficients = jax.scipy.linalg.cho_solve((jnp.linalg.cholesky(total_gram), True), projection.T).T
    restored = jnp.dot(coefficients.astype(jnp.bfloat16).astype(jnp.float32), half_basis.astype(jnp.float32), preferred_element_type=jnp.float32)
    return ((slab_rows.astype(jnp.float32) - restored) * lax.rsqrt(ridge_scale)).astype(jnp.bfloat16)

def reference(activations, ridge_scale):
    block_count = TOK_DEV // (2 * RANK)
    wide_rows = activations.reshape(N_SEQ * block_count, 2 * RANK, D).astype(jnp.float32)
    slab_grams = jnp.einsum('bik,bjk->bij', wide_rows, wide_rows, precision=precise)
    mixtures = jax.vmap(reduce_gram)(slab_grams)
    sketches = jnp.einsum('bij,bjk->bik', mixtures, wide_rows, precision=precise).reshape(N_SEQ, block_count, RANK, D)
    slab_sketch = sketches[:, 0]
    for block_index in range(1, block_count):
        slab_sketch = jax.vmap(combine)(slab_sketch, sketches[:, block_index])
    seq_index = jnp.arange(N_SEQ, dtype=jnp.int32)
    tree_block = slab_sketch
    prefix = slab_sketch
    for tree_level in range(LEVELS):
        sibling = jnp.bitwise_xor(seq_index, jnp.int32(1 << tree_level))
        partner = tree_block[sibling]
        merged = jax.vmap(combine)(partner, prefix)
        has_bit = seq_index // (1 << tree_level) % 2 == 1
        prefix = jnp.where(has_bit[:, None, None], merged, prefix)
        if tree_level + 1 < LEVELS:
            tree_block = jax.vmap(combine)(tree_block, partner)
    seen_rows = ((seq_index + 1) * TOK_DEV).astype(jnp.float32)
    slabs = activations.reshape(N_SEQ, TOK_DEV, D)
    whitened = jax.vmap(whiten, in_axes=(0, 0, 0, None))(slabs, prefix, seen_rows, ridge_scale)
    return whitened.reshape(N_SEQ * TOK_DEV, D)
```

```python
import functools

import jax
import jax.numpy as jnp
from jax import lax
from jax.experimental import pallas as pl
from jax.experimental.pallas import tpu as pltpu
from jax.sharding import PartitionSpec as P

RANK = 128
ROOT_STEPS = 12
HALF = RANK // 2

f32 = jnp.float32
bf16 = jnp.bfloat16
precise = lax.Precision.HIGHEST
ROOT_HALF = 0.7071067811865476


def nn(a, b):
    return lax.dot_general(
        a, b, (((1,), (0,)), ((), ())), precision=precise, preferred_element_type=f32
    )


def nt(a, b):
    return lax.dot_general(
        a, b, (((1,), (1,)), ((), ())), precision=precise, preferred_element_type=f32
    )


def tn(a, b):
    return lax.dot_general(
        a, b, (((0,), (0,)), ((), ())), precision=precise, preferred_element_type=f32
    )


def eye_mask():
    rows = lax.broadcasted_iota(jnp.int32, (RANK, RANK), 0)
    lanes = lax.broadcasted_iota(jnp.int32, (RANK, RANK), 1)
    return rows == lanes


def identity():
    return jnp.where(eye_mask(), 1.0, 0.0).astype(f32)


def trace(matrix):
    return jnp.sum(jnp.where(eye_mask(), matrix, 0.0), keepdims=True)


def parts_of(rows):
    high = rows.astype(bf16).astype(f32)
    rest = rows - high
    middle = rest.astype(bf16).astype(f32)
    return high, middle, rest - middle


def factor(work, upper, last, widths):
    tile = (8, 128)
    sub = lax.broadcasted_iota(jnp.int32, tile, 0)
    lane = lax.broadcasted_iota(jnp.int32, tile, 1)
    count = len(widths)
    for k in range(count):
        last[k] = jnp.zeros_like(last[k])

    def cols(c):
        return slice(128 * c, 128 * c + 128)

    def panel_step(step, carry):
        here = pl.multiple_of(8 * step, 8)
        below = pl.multiple_of(8 * step + 8, 8)
        shift = lax.rem(128 - here, 128)
        panels = [
            [work[k, pl.ds(here, 8), cols(c)] for c in range(widths[k])] for k in range(count)
        ]
        for k in range(count):
            width = 128 * widths[k]
            high, middle, low = parts_of(last[k][:, :width])
            keep = lane >= below
            lh, lm, ll = [jnp.where(keep, part[:, :128], 0.0) for part in (high, middle, low)]
            left = jnp.concatenate([lh, lh, lm, lh, ll, lm], 0).astype(bf16)
            right = jnp.concatenate([high, middle, high, low, high, middle], 0).astype(bf16)
            update = lax.dot_general(
                left, right, (((0,), (0,)), ((), ())), preferred_element_type=f32
            )
            work[k, 0:128, :width] = work[k, 0:128, :width] - update
        for k in range(count):
            block = pltpu.roll(panels[k][0], shift, 1)
            splat = {
                (i, c): jnp.broadcast_to(block[i : i + 1, c : c + 1], tile)
                for i in range(8)
                for c in range(i, 8)
            }
            rows = [
                [jnp.broadcast_to(piece[i : i + 1, :], tile) for i in range(8)]
                for piece in panels[k]
            ]
            scales = []
            for r in range(8):
                scale = lax.rsqrt(splat[r, r])
                scales.append(scale)
                for c in range(r, 8):
                    splat[r, c] = splat[r, c] * scale
                for piece in rows:
                    piece[r] = piece[r] * scale
                for i in range(r + 1, 8):
                    multiplier = splat[r, i]
                    for c in range(i, 8):
                        splat[i, c] = splat[i, c] - multiplier * splat[r, c]
                    for piece in rows:
                        piece[i] = piece[i] - multiplier * piece[r]
            for c, piece in enumerate(rows):
                done = piece[0]
                for r in range(1, 8):
                    done = jnp.where(sub == r, piece[r], done)
                upper[k, pl.ds(here, 8), cols(c)] = done
                last[k, :, cols(c)] = done
            following = [work[k, pl.ds(below, 8), cols(c)] for c in range(widths[k])]
            block = pltpu.roll(following[0], shift, 1)
            heads = [jnp.broadcast_to(block[:, c : c + 1], tile) for c in range(8)]
            for r in range(8):
                multiplier = heads[r] * scales[r]
                for c in range(r + 1, 8):
                    heads[c] = heads[c] - multiplier * splat[r, c]
                for c in range(widths[k]):
                    following[c] = following[c] - multiplier * rows[c][r]
            for c in range(widths[k]):
                work[k, pl.ds(below, 8), cols(c)] = following[c]
        return carry

    lax.fori_loop(0, RANK // 8, panel_step, 0)


def reduce_all(grams, refs):
    work, upper, last = refs
    count = len(grams)
    unit = identity()
    images = []
    for k, (g00, g01, g11) in enumerate(grams):
        top = (g00 + g01) * ROOT_HALF
        low = (g01.T + g11) * ROOT_HALF
        images.append((top, low))
        work[k, 0:128, 0:128] = tn(top, top) + tn(low, low)
        work[k, 0:128, 128:256] = unit
        top_image = nn(g00, top) + nn(g01, low)
        low_image = tn(g01, top) + nn(g11, low)
        work[count + k, 0:128, 0:128] = tn(top, top_image) + tn(low, low_image)
    factor(work, upper, last, [2] * count + [1] * count)
    spans, inners, mixes = [], [], []
    for k, (g00, g01, g11) in enumerate(grams):
        rows = lax.broadcasted_iota(jnp.int32, (RANK, RANK), 0)
        lanes = lax.broadcasted_iota(jnp.int32, (RANK, RANK), 1)
        inverse = upper[k, :, 128:256]
        turned = jnp.where(lanes >= rows, upper[count + k, :, 0:128], 0.0)
        root = nt(turned, inverse)
        inner = nt(root, root)
        top, low = images[k]
        spans.append((root, nt(inverse, top), nt(inverse, low)))
        inners.append(inner)
    for k, (g00, g01, g11) in enumerate(grams):
        tail = (trace(g00) + trace(g11) - trace(inners[k])) / RANK
        work[k, 0:128, 0:128] = inners[k] + tail * unit
        work[k, 0:128, 128:256] = unit
    factor(work, upper, last, [2] * count)
    outs = []
    for k in range(count):
        root, first, second = spans[k]
        inverse = upper[k, :, 128:256]
        shrunk = nn(inverse, root)
        square = nn(inverse, inners[k])
        outs.append((nn(shrunk, first), nn(shrunk, second), nt(square, square)))
    return outs


def scratch(count):
    return [
        pltpu.VMEM((2 * count, RANK + 8, 256), f32),
        pltpu.VMEM((2 * count, RANK, 256), f32),
        pltpu.VMEM((2 * count, 8, 256), f32),
    ]


def on_core(kernel, outs, scratches, *operands):
    vmem = pl.BlockSpec(memory_space=pltpu.VMEM)
    return pl.pallas_call(
        kernel,
        out_shape=[jax.ShapeDtypeStruct(shape, dtype) for shape, dtype in outs],
        in_specs=[vmem] * len(operands),
        out_specs=[vmem] * len(outs),
        scratch_shapes=scratches,
        compiler_params=pltpu.CompilerParams(vmem_limit_bytes=40 << 20),
    )(*operands)


def slab_gram_kernel(own, other, out):
    mine = own[...]
    theirs = other[...].astype(bf16)
    dims = (((1,), (1,)), ((), ()))
    out[0:256] = lax.dot_general(mine, mine, dims, preferred_element_type=f32)
    out[256:512] = lax.dot_general(mine, theirs, dims, preferred_element_type=f32)
    out[512:768] = lax.dot_general(theirs, theirs, dims, preferred_element_type=f32)


def quarters(ref, start):
    return (
        ref[start : start + 128, 0:128],
        ref[start : start + 128, 128:256],
        ref[start + 128 : start + 256, 128:256],
    )


def slab_kernel(facts, gram, own, other, block, prefix, work, upper, last):
    refs = (work, upper, last)
    mine, theirs = reduce_all([quarters(gram, 0), quarters(gram, 512)], refs)
    cross = gram[256:512]
    across = nn(mine[0], cross[0:128]) + nn(mine[1], cross[128:256])
    across = nt(across[:, 0:128], theirs[0]) + nt(across[:, 128:256], theirs[1])
    ((first, second, _),) = reduce_all([(mine[2], across, theirs[2])], refs)
    rows = own[...].astype(f32)
    own_sketch = nn(mine[0], rows[0:128]) + nn(mine[1], rows[128:256])
    rows = other[...]
    other_sketch = nn(theirs[0], rows[0:128]) + nn(theirs[1], rows[128:256])
    merged = nn(first, own_sketch) + nn(second, other_sketch)
    block[...] = merged
    prefix[...] = jnp.where(facts[0:1, 0:1] > 0.5, merged, own_sketch)


def whole(core, kept, swapped):
    top = jnp.where(core, swapped, kept)
    low = jnp.where(core, kept, swapped)
    return jnp.concatenate([top, low], 0)


INNER = ((0, 0), (1, 1), (2, 2), (3, 3), (4, 4), (0, 1), (2, 3), (1, 4), (0, 2), (0, 3),
         (1, 2), (1, 3), (2, 4), (3, 4))
OUTER = tuple(pair for pair in INNER if 0 not in pair)


def gram_kernel(pairs, with_rows, facts, kept, swapped, block, prefix, *rest):
    rows, (grams, peers) = (rest[0], rest[1:]) if with_rows else (None, rest)
    core = facts[2:3, 0:1] > 0.5
    sketches = [block[...]]
    for j in range(3):
        sketches.append(whole(core, kept[j], swapped[j]))
        peers[j] = sketches[-1]
    sketches.append(prefix[...])
    for place, (a, b) in enumerate(pairs):
        grams[128 * place : 128 * place + 128] = nt(sketches[a], sketches[b])
    if with_rows:
        own = rows[...].astype(f32)
        for place, a in enumerate((2, 3, 1, 4)):
            start = 128 * len(pairs) + 256 * place
            grams[start : start + 256] = nt(own, sketches[a])


def merge_prefix(take_near, blocks, far, near, prefix_gram):
    unit = identity()
    first = jnp.where(take_near, near[0], 0.0)
    second = jnp.where(take_near, near[1], unit)
    gram = jnp.where(take_near, near[2], prefix_gram)
    with_near = nn(far[0], blocks[1, 2].T) + nn(far[1], blocks[1, 3].T)
    with_prefix = nn(far[0], blocks[2, 4]) + nn(far[1], blocks[3, 4])
    across = nt(with_near, first) + nt(with_prefix, second)
    return first, second, gram, across


def combine_prefix(take_far, far, near_first, near_second, merged):
    first, second = merged[0], merged[1]
    return (
        jnp.where(take_far, nn(first, far[0]), 0.0),
        jnp.where(take_far, nn(first, far[1]), 0.0),
        jnp.where(take_far, nn(second, near_first), near_first),
        jnp.where(take_far, nn(second, near_second), near_second),
    )


def inner_kernel(facts, gram, block, peers, prefix, new_block, new_prefix, work, upper, last):
    refs = (work, upper, last)
    blocks = {pair: gram[128 * n : 128 * n + 128] for n, pair in enumerate(INNER)}
    take_near, take_far = facts[0:1, 0:1] > 0.5, facts[1:2, 0:1] > 0.5
    pair_of, far, near = reduce_all(
        [
            (blocks[0, 0], blocks[0, 1], blocks[1, 1]),
            (blocks[2, 2], blocks[2, 3], blocks[3, 3]),
            (blocks[1, 1], blocks[1, 4], blocks[4, 4]),
        ],
        refs,
    )
    left = nn(pair_of[0], blocks[0, 2]) + nn(pair_of[1], blocks[1, 2])
    right = nn(pair_of[0], blocks[0, 3]) + nn(pair_of[1], blocks[1, 3])
    across_blocks = nt(left, far[0]) + nt(right, far[1])
    near_first, near_second, prefix_gram, across = merge_prefix(
        take_near, blocks, far, near, blocks[4, 4]
    )
    merged_block, merged = reduce_all(
        [(pair_of[2], across_blocks, far[2]), (far[2], across, prefix_gram)], refs
    )
    own, mine = block[...], prefix[...]
    near_peer, far_a, far_b = peers[0], peers[1], peers[2]
    near_pair = nn(pair_of[0], own) + nn(pair_of[1], near_peer)
    far_pair = nn(far[0], far_a) + nn(far[1], far_b)
    new_block[...] = nn(merged_block[0], near_pair) + nn(merged_block[1], far_pair)
    c2, c3, c1, c4 = combine_prefix(take_far, far, near_first, near_second, merged)
    new_prefix[...] = nn(c2, far_a) + nn(c3, far_b) + nn(c1, near_peer) + nn(c4, mine)


def outer_kernel(facts, gram, peers, prefix, rows, out, work, upper, last):
    refs = (work, upper, last)
    blocks = {pair: gram[128 * n : 128 * n + 128] for n, pair in enumerate(OUTER)}
    take_near, take_far = facts[0:1, 0:1] > 0.5, facts[1:2, 0:1] > 0.5
    far, near = reduce_all(
        [
            (blocks[2, 2], blocks[2, 3], blocks[3, 3]),
            (blocks[1, 1], blocks[1, 4], blocks[4, 4]),
        ],
        refs,
    )
    near_first, near_second, prefix_gram, across = merge_prefix(
        take_near, blocks, far, near, blocks[4, 4]
    )
    (merged,) = reduce_all([(far[2], across, prefix_gram)], refs)
    scale = facts[3:4, 0:1]
    coefs = combine_prefix(take_far, far, near_first, near_second, merged)
    coefs = [c * scale for c in coefs]
    sketches = [peers[1], peers[2], peers[0], prefix[...]]
    scaled = sum(nn(c, sketch) for c, sketch in zip(coefs, sketches))
    half_basis = scaled.astype(bf16)
    start = 128 * len(OUTER)
    projection = sum(
        nt(gram[start + 256 * n : start + 256 * n + 256], c) for n, c in enumerate(coefs)
    )
    unit = identity()
    small = jnp.where(take_far, merged[2], prefix_gram) * (scale * scale)
    shifted = unit + small
    size = jnp.sqrt(jnp.sum(shifted * shifted, keepdims=True))
    current = shifted / size
    partner = unit
    for repeat in range(ROOT_STEPS):
        middle = 1.5 * unit - 0.5 * (nn(partner, current) if repeat else current)
        current = nn(current, middle)
        if repeat + 1 < ROOT_STEPS:
            partner = nn(middle, partner) if repeat else middle
    total = shifted + current * jnp.sqrt(size)
    total = 0.5 * (total + total.T)
    work[0, 0:128, 0:128] = total
    work[0, 0:128, 128:256] = unit
    factor(work, upper, last, [2])
    inverse = upper[0, :, 128:256]
    coefficients = nn(nt(projection, inverse), inverse)
    restored = jnp.dot(coefficients.astype(bf16), half_basis, preferred_element_type=f32)
    out[...] = ((rows[...].astype(f32) - restored) * facts[4:5, 0:1]).astype(bf16)


def over_features(partial):
    count = lax.axis_size("feat")
    share, width = partial.shape[0] // count, partial.shape[1]
    pieces = lax.all_to_all(
        partial.reshape(count, share, width), "feat", split_axis=0, concat_axis=0, tiled=True
    )
    total = jnp.sum(pieces, axis=0)
    copies = jnp.broadcast_to(total, (count, share, width))
    everything = lax.all_to_all(copies, "feat", split_axis=0, concat_axis=0, tiled=True)
    return everything.reshape(count * share, width)


def from_partner(block, flips, wanted=None):
    route = [
        (s, s ^ flips)
        for s in range(lax.axis_size("seq"))
        if wanted is None or (s ^ flips) & wanted == wanted
    ]
    return lax.ppermute(block, "seq", route)


def peers_of(block, near, far, core, one_way):
    half = lax.dynamic_slice_in_dim(block, core * HALF, HALF, 0)
    kept = jnp.stack(
        [
            from_partner(half, near, near if one_way else None),
            from_partner(half, far, far if one_way else None),
            from_partner(half, near | far, far if one_way else None),
        ]
    )
    return kept, from_partner(kept, 1)


def on_device(activations, ridge_scale):
    seq_index = lax.axis_index("seq")
    width = activations.shape[1]
    core = seq_index % 2
    seen_rows = ((seq_index + 1) * activations.shape[0]).astype(f32)

    def facts_of(near, far):
        values = [
            (seq_index // near % 2).astype(f32),
            (seq_index // far % 2).astype(f32),
            core.astype(f32),
            lax.rsqrt(seen_rows * ridge_scale),
            lax.rsqrt(ridge_scale),
        ]
        values += [jnp.zeros((), f32)] * 3
        return jnp.broadcast_to(jnp.stack(values)[:, None], (8, 128))

    other = from_partner(activations.astype(f32), 1)
    (partial,) = on_core(slab_gram_kernel, [((768, 256), f32)], [], activations, other)
    gram = over_features(partial)
    sketch = ((RANK, width), f32)
    block, prefix = on_core(
        slab_kernel, [sketch, sketch], scratch(2), facts_of(1, 1), gram, activations, other
    )

    facts = facts_of(2, 4)
    kept, swapped = peers_of(block, 2, 4, core, False)
    partial, peers = on_core(
        functools.partial(gram_kernel, INNER, False),
        [((128 * len(INNER), 128), f32), ((3, RANK, width), f32)],
        [],
        facts, kept, swapped, block, prefix,
    )
    gram = over_features(partial)
    block, prefix = on_core(
        inner_kernel, [sketch, sketch], scratch(3), facts, gram, block, peers, prefix
    )

    facts = facts_of(8, 16)
    kept, swapped = peers_of(block, 8, 16, core, True)
    partial, peers = on_core(
        functools.partial(gram_kernel, OUTER, True),
        [((128 * (len(OUTER) + 8), 128), f32), ((3, RANK, width), f32)],
        [],
        facts, kept, swapped, block, prefix, activations,
    )
    gram = over_features(partial)
    (whitened,) = on_core(
        outer_kernel,
        [(activations.shape, bf16)],
        scratch(2),
        facts, gram, peers, prefix, activations,
    )
    return whitened


def solution(mesh):
    placed = (P("seq", "feat"), P())
    return jax.shard_map(
        on_device, mesh=mesh, in_specs=placed, out_specs=P("seq", "feat"), check_vma=False
    )
```

```python
import functools

import jax
import jax.numpy as jnp
from jax import lax
from jax.experimental import pallas as pl
from jax.experimental.pallas import tpu as pltpu
from jax.sharding import PartitionSpec as P

RANK = 128
ROOT_STEPS = 12
HALF = RANK // 2

f32 = jnp.float32
bf16 = jnp.bfloat16
precise = lax.Precision.HIGHEST
ROOT_HALF = 0.7071067811865476


def nn(a, b):
    return lax.dot_general(
        a, b, (((1,), (0,)), ((), ())), precision=precise, preferred_element_type=f32
    )


def nt(a, b):
    return lax.dot_general(
        a, b, (((1,), (1,)), ((), ())), precision=precise, preferred_element_type=f32
    )


def tn(a, b):
    return lax.dot_general(
        a, b, (((0,), (0,)), ((), ())), precision=precise, preferred_element_type=f32
    )


def eye_mask():
    rows = lax.broadcasted_iota(jnp.int32, (RANK, RANK), 0)
    lanes = lax.broadcasted_iota(jnp.int32, (RANK, RANK), 1)
    return rows == lanes


def identity():
    return jnp.where(eye_mask(), 1.0, 0.0).astype(f32)


def trace(matrix):
    return jnp.sum(jnp.where(eye_mask(), matrix, 0.0), keepdims=True)


def parts_of(rows):
    high = rows.astype(bf16).astype(f32)
    rest = rows - high
    middle = rest.astype(bf16).astype(f32)
    return high, middle, rest - middle


def factor(work, upper, last, widths):
    tile = (8, 128)
    sub = lax.broadcasted_iota(jnp.int32, tile, 0)
    lane = lax.broadcasted_iota(jnp.int32, tile, 1)
    count = len(widths)
    for k in range(count):
        last[k] = jnp.zeros_like(last[k])

    def cols(c):
        return slice(128 * c, 128 * c + 128)

    def panel_step(step, carry):
        here = pl.multiple_of(8 * step, 8)
        below = pl.multiple_of(8 * step + 8, 8)
        shift = lax.rem(128 - here, 128)
        panels = [
            [work[k, pl.ds(here, 8), cols(c)] for c in range(widths[k])] for k in range(count)
        ]
        for k in range(count):
            width = 128 * widths[k]
            high, middle, low = parts_of(last[k][:, :width])
            keep = lane >= below
            lh, lm, ll = [jnp.where(keep, part[:, :128], 0.0) for part in (high, middle, low)]
            left = jnp.concatenate([lh, lh, lm, lh, ll, lm], 0).astype(bf16)
            right = jnp.concatenate([high, middle, high, low, high, middle], 0).astype(bf16)
            update = lax.dot_general(
                left, right, (((0,), (0,)), ((), ())), preferred_element_type=f32
            )
            work[k, 0:128, :width] = work[k, 0:128, :width] - update
        for k in range(count):
            block = pltpu.roll(panels[k][0], shift, 1)
            splat = {
                (i, c): jnp.broadcast_to(block[i : i + 1, c : c + 1], tile)
                for i in range(8)
                for c in range(i, 8)
            }
            rows = [
                [jnp.broadcast_to(piece[i : i + 1, :], tile) for i in range(8)]
                for piece in panels[k]
            ]
            scales = []
            for r in range(8):
                scale = lax.rsqrt(splat[r, r])
                scales.append(scale)
                for c in range(r, 8):
                    splat[r, c] = splat[r, c] * scale
                for piece in rows:
                    piece[r] = piece[r] * scale
                for i in range(r + 1, 8):
                    multiplier = splat[r, i]
                    for c in range(i, 8):
                        splat[i, c] = splat[i, c] - multiplier * splat[r, c]
                    for piece in rows:
                        piece[i] = piece[i] - multiplier * piece[r]
            for c, piece in enumerate(rows):
                done = piece[0]
                for r in range(1, 8):
                    done = jnp.where(sub == r, piece[r], done)
                upper[k, pl.ds(here, 8), cols(c)] = done
                last[k, :, cols(c)] = done
            following = [work[k, pl.ds(below, 8), cols(c)] for c in range(widths[k])]
            block = pltpu.roll(following[0], shift, 1)
            heads = [jnp.broadcast_to(block[:, c : c + 1], tile) for c in range(8)]
            for r in range(8):
                multiplier = heads[r] * scales[r]
                for c in range(r + 1, 8):
                    heads[c] = heads[c] - multiplier * splat[r, c]
                for c in range(widths[k]):
                    following[c] = following[c] - multiplier * rows[c][r]
            for c in range(widths[k]):
                work[k, pl.ds(below, 8), cols(c)] = following[c]
        return carry

    lax.fori_loop(0, RANK // 8, panel_step, 0)


def reduce_all(grams, refs):
    work, upper, last = refs
    count = len(grams)
    unit = identity()
    images = []
    for k, (g00, g01, g11) in enumerate(grams):
        stacked = whole_gram(g00, g01, g01.T, g11)
        image = (stacked[:, 0:128] + stacked[:, 128:256]) * ROOT_HALF
        images.append(image)
        products = tn(image, jnp.concatenate([image, nn(stacked, image)], 1))
        work[k, 0:128, 0:128] = products[:, 0:128]
        work[k, 0:128, 128:256] = unit
        work[count + k, 0:128, 0:128] = products[:, 128:256]
    factor(work, upper, last, [2] * count + [1] * count)
    rows = lax.broadcasted_iota(jnp.int32, (RANK, RANK), 0)
    lanes = lax.broadcasted_iota(jnp.int32, (RANK, RANK), 1)
    roots, inners, spans = [], [], []
    for k, (g00, g01, g11) in enumerate(grams):
        inverse = upper[k, :, 128:256]
        turned = jnp.where(lanes >= rows, upper[count + k, :, 0:128], 0.0)
        root = nt(turned, inverse)
        inner = nt(root, root)
        tail = (trace(g00) + trace(g11) - trace(inner)) / RANK
        work[k, 0:128, 0:128] = inner + tail * unit
        work[k, 0:128, 128:256] = unit
        roots.append(root)
        inners.append(inner)
        spans.append(nt(inverse, images[k]))
    factor(work, upper, last, [2] * count)
    outs = []
    for k in range(count):
        inverse = upper[k, :, 128:256]
        both = nn(inverse, jnp.concatenate([roots[k], inners[k]], 1))
        square = both[:, 128:256]
        outs.append((nn(both[:, 0:128], spans[k]), nt(square, square)))
    return outs


def whole_gram(g00, g01, g10, g11):
    return jnp.concatenate(
        [jnp.concatenate([g00, g01], 1), jnp.concatenate([g10, g11], 1)], 0
    )


def scratch(count):
    return [
        pltpu.VMEM((2 * count, RANK + 8, 256), f32),
        pltpu.VMEM((2 * count, RANK, 256), f32),
        pltpu.VMEM((2 * count, 8, 256), f32),
    ]


def on_core(kernel, outs, scratches, *operands):
    vmem = pl.BlockSpec(memory_space=pltpu.VMEM)
    return pl.pallas_call(
        kernel,
        out_shape=[jax.ShapeDtypeStruct(shape, dtype) for shape, dtype in outs],
        in_specs=[vmem] * len(operands),
        out_specs=[vmem] * len(outs),
        scratch_shapes=scratches,
        compiler_params=pltpu.CompilerParams(vmem_limit_bytes=40 << 20),
    )(*operands)


SLAB = ((0, 0), (0, 1), (1, 1), (2, 2), (2, 3), (3, 3), (0, 2), (0, 3), (1, 2), (1, 3))


def slab_gram_kernel(own, other, out):
    rows = jnp.concatenate([own[...], other[...].astype(bf16)], 0)
    gram = lax.dot_general(rows, rows, (((1,), (1,)), ((), ())), preferred_element_type=f32)
    for place, (a, b) in enumerate(SLAB):
        out[128 * place : 128 * place + 128] = gram[
            128 * a : 128 * a + 128, 128 * b : 128 * b + 128
        ]


def blocks_of(gram, pairs):
    return {pair: gram[128 * n : 128 * n + 128] for n, pair in enumerate(pairs)}


def slab_kernel(
    facts, gram, own, other, block, prefix, block_gram, prefix_gram, work, upper, last
):
    refs = (work, upper, last)
    g = blocks_of(gram, SLAB)
    (mine, my_gram), (theirs, their_gram) = reduce_all(
        [(g[0, 0], g[0, 1], g[1, 1]), (g[2, 2], g[2, 3], g[3, 3])], refs
    )
    across = nt(nn(mine, whole_gram(g[0, 2], g[0, 3], g[1, 2], g[1, 3])), theirs)
    ((mixing, merged_gram),) = reduce_all([(my_gram, across, their_gram)], refs)
    own_sketch = nn(mine, own[...].astype(f32))
    other_sketch = nn(theirs, other[...])
    merged = nn(mixing, jnp.concatenate([own_sketch, other_sketch], 0))
    take = facts[0:1, 0:1] > 0.5
    block[...] = merged
    block_gram[...] = merged_gram
    prefix[...] = jnp.where(take, merged, own_sketch)
    prefix_gram[...] = jnp.where(take, merged_gram, my_gram)


def whole(core, kept, swapped):
    top = jnp.where(core, swapped, kept)
    low = jnp.where(core, kept, swapped)
    return jnp.concatenate([top, low], 0)


OUTER = ((1, 1), (1, 2), (1, 3), (1, 4), (2, 2), (2, 3), (2, 4), (3, 3), (3, 4))
INNER = OUTER + ((0, 1), (0, 2), (0, 3))


def gram_kernel(with_rows, facts, kept, swapped, block, prefix, *rest):
    rows, (grams, peers) = (rest[0], rest[1:]) if with_rows else (None, rest)
    core = facts[2:3, 0:1] > 0.5
    sketches = [block[...]]
    for j in range(3):
        sketches.append(whole(core, kept[j], swapped[j]))
        peers[j] = sketches[-1]
    sketches.append(prefix[...])

    def put(place, left, right):
        product = nt(left, jnp.concatenate(right, 0))
        size = left.shape[0]
        for n in range(len(right)):
            grams[place : place + size] = product[:, 128 * n : 128 * n + 128]
            place += size
        return place

    place = put(0, sketches[1], sketches[1:5])
    place = put(place, sketches[2], sketches[2:5])
    place = put(place, sketches[3], sketches[3:5])
    if with_rows:
        put(place, rows[...].astype(f32), [sketches[a] for a in (2, 3, 1, 4)])
    else:
        put(place, sketches[0], sketches[1:4])


def merge_prefix(take_near, g, far, near, near_gram, prefix_gram):
    unit = identity()
    mixing = jnp.where(take_near, near, jnp.concatenate([jnp.zeros_like(unit), unit], 1))
    gram = jnp.where(take_near, near_gram, prefix_gram)
    with_rows = nn(far, whole_gram(g[1, 2].T, g[2, 4], g[1, 3].T, g[3, 4]))
    return mixing, gram, nt(with_rows, mixing)


def combine_prefix(take_far, far, near, merged):
    first = jnp.where(take_far, nn(merged[:, 0:128], far), 0.0)
    second = jnp.where(take_far, nn(merged[:, 128:256], near), near)
    return jnp.concatenate([first, second], 1)


def inner_kernel(
    facts, gram, block, peers, prefix, block_gram, prefix_gram,
    new_block, new_prefix, new_prefix_gram, work, upper, last,
):
    refs = (work, upper, last)
    g = blocks_of(gram, INNER)
    take_near, take_far = facts[0:1, 0:1] > 0.5, facts[1:2, 0:1] > 0.5
    (pair, pair_gram), (far, far_gram), (near, near_gram) = reduce_all(
        [
            (block_gram[...], g[0, 1], g[1, 1]),
            (g[2, 2], g[2, 3], g[3, 3]),
            (g[1, 1], g[1, 4], prefix_gram[...]),
        ],
        refs,
    )
    across_blocks = nt(nn(pair, whole_gram(g[0, 2], g[0, 3], g[1, 2], g[1, 3])), far)
    near, near_gram, across = merge_prefix(
        take_near, g, far, near, near_gram, prefix_gram[...]
    )
    (merged_block, _), (merged, merged_gram) = reduce_all(
        [(pair_gram, across_blocks, far_gram), (far_gram, across, near_gram)], refs
    )
    own_pair = jnp.concatenate([block[...], peers[0]], 0)
    far_pair = jnp.concatenate([peers[1], peers[2]], 0)
    halves = jnp.concatenate([nn(pair, own_pair), nn(far, far_pair)], 0)
    new_block[...] = nn(merged_block, halves)
    coefs = combine_prefix(take_far, far, near, merged)
    new_prefix[...] = nn(coefs, jnp.concatenate([far_pair, peers[0], prefix[...]], 0))
    new_prefix_gram[...] = jnp.where(take_far, merged_gram, near_gram)


def outer_kernel(facts, gram, peers, prefix, prefix_gram, rows, out, work, upper, last):
    refs = (work, upper, last)
    g = blocks_of(gram, OUTER)
    take_near, take_far = facts[0:1, 0:1] > 0.5, facts[1:2, 0:1] > 0.5
    (far, far_gram), (near, near_gram) = reduce_all(
        [
            (g[2, 2], g[2, 3], g[3, 3]),
            (g[1, 1], g[1, 4], prefix_gram[...]),
        ],
        refs,
    )
    near, near_gram, across = merge_prefix(
        take_near, g, far, near, near_gram, prefix_gram[...]
    )
    ((merged, merged_gram),) = reduce_all([(far_gram, across, near_gram)], refs)
    scale = facts[3:4, 0:1]
    coefs = combine_prefix(take_far, far, near, merged) * scale
    scaled = nn(coefs, jnp.concatenate([peers[1], peers[2], peers[0], prefix[...]], 0))
    half_basis = scaled.astype(bf16)
    start = 128 * len(OUTER)
    projection = nt(
        jnp.concatenate([gram[start + 256 * n : start + 256 * n + 256] for n in range(4)], 1),
        coefs,
    )
    unit = identity()
    shifted = unit + jnp.where(take_far, merged_gram, near_gram) * (scale * scale)
    size = jnp.sqrt(jnp.sum(shifted * shifted, keepdims=True))
    current = shifted / size
    partner = unit
    for repeat in range(ROOT_STEPS):
        middle = 1.5 * unit - 0.5 * (nn(partner, current) if repeat else current)
        current = nn(current, middle)
        if repeat + 1 < ROOT_STEPS:
            partner = nn(middle, partner) if repeat else middle
    total = shifted + current * jnp.sqrt(size)
    total = 0.5 * (total + total.T)
    work[0, 0:128, 0:128] = total
    work[0, 0:128, 128:256] = unit
    factor(work, upper, last, [2])
    inverse = upper[0, :, 128:256]
    coefficients = nn(nt(projection, inverse), inverse)
    restored = jnp.dot(coefficients.astype(bf16), half_basis, preferred_element_type=f32)
    out[...] = ((rows[...].astype(f32) - restored) * facts[4:5, 0:1]).astype(bf16)


def over_features(partial):
    count = lax.axis_size("feat")
    share, width = partial.shape[0] // count, partial.shape[1]
    pieces = lax.all_to_all(
        partial.reshape(count, share, width), "feat", split_axis=0, concat_axis=0, tiled=True
    )
    total = jnp.sum(pieces, axis=0)
    copies = jnp.broadcast_to(total, (count, share, width))
    everything = lax.all_to_all(copies, "feat", split_axis=0, concat_axis=0, tiled=True)
    return everything.reshape(count * share, width)


def from_partner(block, flips, wanted=None):
    route = [
        (s, s ^ flips)
        for s in range(lax.axis_size("seq"))
        if wanted is None or (s ^ flips) & wanted == wanted
    ]
    return lax.ppermute(block, "seq", route)


def peers_of(block, near, far, core, one_way):
    half = lax.dynamic_slice_in_dim(block, core * HALF, HALF, 0)
    kept = jnp.stack(
        [
            from_partner(half, near, near if one_way else None),
            from_partner(half, far, far if one_way else None),
            from_partner(half, near | far, far if one_way else None),
        ]
    )
    return kept, from_partner(kept, 1)


def on_device(activations, ridge_scale):
    seq_index = lax.axis_index("seq")
    width = activations.shape[1]
    core = seq_index % 2
    seen_rows = ((seq_index + 1) * activations.shape[0]).astype(f32)

    def facts_of(near, far):
        values = [
            (seq_index // near % 2).astype(f32),
            (seq_index // far % 2).astype(f32),
            core.astype(f32),
            lax.rsqrt(seen_rows * ridge_scale),
            lax.rsqrt(ridge_scale),
        ]
        values += [jnp.zeros((), f32)] * 3
        return jnp.broadcast_to(jnp.stack(values)[:, None], (8, 128))

    other = from_partner(activations.astype(f32), 1)
    (partial,) = on_core(
        slab_gram_kernel, [((128 * len(SLAB), 128), f32)], [], activations, other
    )
    gram = over_features(partial)
    sketch, square = ((RANK, width), f32), ((RANK, RANK), f32)
    block, prefix, block_gram, prefix_gram = on_core(
        slab_kernel,
        [sketch, sketch, square, square],
        scratch(2),
        facts_of(1, 1), gram, activations, other,
    )

    facts = facts_of(2, 4)
    kept, swapped = peers_of(block, 2, 4, core, False)
    partial, peers = on_core(
        functools.partial(gram_kernel, False),
        [((128 * len(INNER), 128), f32), ((3, RANK, width), f32)],
        [],
        facts, kept, swapped, block, prefix,
    )
    gram = over_features(partial)
    block, prefix, prefix_gram = on_core(
        inner_kernel,
        [sketch, sketch, square],
        scratch(3),
        facts, gram, block, peers, prefix, block_gram, prefix_gram,
    )

    facts = facts_of(8, 16)
    kept, swapped = peers_of(block, 8, 16, core, True)
    partial, peers = on_core(
        functools.partial(gram_kernel, True),
        [((128 * (len(OUTER) + 8), 128), f32), ((3, RANK, width), f32)],
        [],
        facts, kept, swapped, block, prefix, activations,
    )
    gram = over_features(partial)
    (whitened,) = on_core(
        outer_kernel,
        [(activations.shape, bf16)],
        scratch(2),
        facts, gram, peers, prefix, prefix_gram, activations,
    )
    return whitened


def solution(mesh):
    placed = (P("seq", "feat"), P())
    return jax.shard_map(
        on_device, mesh=mesh, in_specs=placed, out_specs=P("seq", "feat"), check_vma=False
    )
```

```python
import functools

import jax
import jax.numpy as jnp
from jax import lax
from jax.experimental import pallas as pl
from jax.experimental.pallas import tpu as pltpu
from jax.sharding import PartitionSpec as P

RANK = 128
ROOT_STEPS = 12
HALF = RANK // 2

f32 = jnp.float32
bf16 = jnp.bfloat16
precise = lax.Precision.HIGHEST
ROOT_HALF = 0.7071067811865476


def nn(a, b):
    return lax.dot_general(
        a, b, (((1,), (0,)), ((), ())), precision=precise, preferred_element_type=f32
    )


def nt(a, b):
    return lax.dot_general(
        a, b, (((1,), (1,)), ((), ())), precision=precise, preferred_element_type=f32
    )


def tn(a, b):
    return lax.dot_general(
        a, b, (((0,), (0,)), ((), ())), precision=precise, preferred_element_type=f32
    )


def eye_mask():
    rows = lax.broadcasted_iota(jnp.int32, (RANK, RANK), 0)
    lanes = lax.broadcasted_iota(jnp.int32, (RANK, RANK), 1)
    return rows == lanes


def identity():
    return jnp.where(eye_mask(), 1.0, 0.0).astype(f32)


def trace(matrix):
    return jnp.sum(jnp.where(eye_mask(), matrix, 0.0), keepdims=True)


def parts_of(rows):
    high = rows.astype(bf16).astype(f32)
    rest = rows - high
    middle = rest.astype(bf16).astype(f32)
    return high, middle, rest - middle


def factor(work, upper, last, widths):
    if len(widths) <= 2:
        return factor_by_pairs(work, upper, widths)
    tile = (8, 128)
    sub = lax.broadcasted_iota(jnp.int32, tile, 0)
    lane = lax.broadcasted_iota(jnp.int32, tile, 1)
    count = len(widths)
    for k in range(count):
        last[k] = jnp.zeros_like(last[k])

    def cols(c):
        return slice(128 * c, 128 * c + 128)

    def panel_step(step, carry):
        here = pl.multiple_of(8 * step, 8)
        below = pl.multiple_of(8 * step + 8, 8)
        shift = lax.rem(128 - here, 128)
        panels = [
            [work[k, pl.ds(here, 8), cols(c)] for c in range(widths[k])] for k in range(count)
        ]
        for k in range(count):
            width = 128 * widths[k]
            high, middle, low = parts_of(last[k][:, :width])
            keep = lane >= below
            lh, lm, ll = [jnp.where(keep, part[:, :128], 0.0) for part in (high, middle, low)]
            left = jnp.concatenate([lh, lh, lm, lh, ll, lm], 0).astype(bf16)
            right = jnp.concatenate([high, middle, high, low, high, middle], 0).astype(bf16)
            update = lax.dot_general(
                left, right, (((0,), (0,)), ((), ())), preferred_element_type=f32
            )
            work[k, 0:128, :width] = work[k, 0:128, :width] - update
        for k in range(count):
            block = pltpu.roll(panels[k][0], shift, 1)
            splat = {
                (i, c): jnp.broadcast_to(block[i : i + 1, c : c + 1], tile)
                for i in range(8)
                for c in range(i, 8)
            }
            rows = [
                [jnp.broadcast_to(piece[i : i + 1, :], tile) for i in range(8)]
                for piece in panels[k]
            ]
            scales = []
            for r in range(8):
                scale = lax.rsqrt(splat[r, r])
                scales.append(scale)
                for c in range(r, 8):
                    splat[r, c] = splat[r, c] * scale
                for piece in rows:
                    piece[r] = piece[r] * scale
                for i in range(r + 1, 8):
                    multiplier = splat[r, i]
                    for c in range(i, 8):
                        splat[i, c] = splat[i, c] - multiplier * splat[r, c]
                    for piece in rows:
                        piece[i] = piece[i] - multiplier * piece[r]
            for c, piece in enumerate(rows):
                done = piece[0]
                for r in range(1, 8):
                    done = jnp.where(sub == r, piece[r], done)
                upper[k, pl.ds(here, 8), cols(c)] = done
                last[k, :, cols(c)] = done
            following = [work[k, pl.ds(below, 8), cols(c)] for c in range(widths[k])]
            block = pltpu.roll(following[0], shift, 1)
            heads = [jnp.broadcast_to(block[:, c : c + 1], tile) for c in range(8)]
            for r in range(8):
                multiplier = heads[r] * scales[r]
                for c in range(r + 1, 8):
                    heads[c] = heads[c] - multiplier * splat[r, c]
                for c in range(widths[k]):
                    following[c] = following[c] - multiplier * rows[c][r]
            for c in range(widths[k]):
                work[k, pl.ds(below, 8), cols(c)] = following[c]
        return carry

    lax.fori_loop(0, RANK // 8, panel_step, 0)


def lockstep(steps):
    steps, results = list(steps), {}
    live = list(range(len(steps)))
    while live:
        for i in list(live):
            try:
                next(steps[i])
            except StopIteration as stop:
                results[i] = stop.value
                live.remove(i)
    return [results[i] for i in range(len(steps))]


def eliminate(pieces, shift):
    tile = (8, 128)
    sub = lax.broadcasted_iota(jnp.int32, tile, 0)
    block = pltpu.roll(pieces[0], shift, 1)
    splat = {
        (i, c): jnp.broadcast_to(block[i : i + 1, c : c + 1], tile)
        for i in range(8)
        for c in range(i, 8)
    }
    rows = [[jnp.broadcast_to(piece[i : i + 1, :], tile) for i in range(8)] for piece in pieces]
    scales = []
    yield
    for r in range(8):
        scale = lax.rsqrt(splat[r, r])
        scales.append(scale)
        for c in range(r, 8):
            splat[r, c] = splat[r, c] * scale
        for piece in rows:
            piece[r] = piece[r] * scale
        for i in range(r + 1, 8):
            multiplier = splat[r, i]
            for c in range(i, 8):
                splat[i, c] = splat[i, c] - multiplier * splat[r, c]
            for piece in rows:
                piece[i] = piece[i] - multiplier * piece[r]
        yield
    done = []
    for piece in rows:
        merged = piece[0]
        for r in range(1, 8):
            merged = jnp.where(sub == r, piece[r], merged)
        done.append(merged)
    return splat, rows, scales, done


def update(pieces, shift, factored):
    splat, rows, scales, _ = factored
    block = pltpu.roll(pieces[0], shift, 1)
    heads = [jnp.broadcast_to(block[:, c : c + 1], (8, 128)) for c in range(8)]
    pieces = list(pieces)
    yield
    for r in range(8):
        multiplier = heads[r] * scales[r]
        for c in range(r + 1, 8):
            heads[c] = heads[c] - multiplier * splat[r, c]
        for c in range(len(pieces)):
            pieces[c] = pieces[c] - multiplier * rows[c][r]
        yield
    return pieces


def factor_by_pairs(work, upper, widths):
    count = len(widths)
    every = range(count)
    lane = lax.broadcasted_iota(jnp.int32, (16, 128), 1)

    def load(k, start):
        return [work[k, pl.ds(start, 8), 128 * c : 128 * c + 128] for c in range(widths[k])]

    def pair_step(step, carry):
        before, panels = carry
        here = pl.multiple_of(16 * step, 16)
        below = pl.multiple_of(16 * step + 16, 16)
        shift_a, shift_b = lax.rem(128 - here, 128), lax.rem(248 - here, 128)
        for k in every:
            width = 128 * widths[k]
            high, middle, low = parts_of(before[k])
            keep = lane >= below
            lh, lm, ll = [jnp.where(keep, part[:, :128], 0.0) for part in (high, middle, low)]
            left = jnp.concatenate([lh, lh, lm, lh, ll, lm], 0).astype(bf16)
            right = jnp.concatenate([high, middle, high, low, high, middle], 0).astype(bf16)
            change = lax.dot_general(
                left, right, (((0,), (0,)), ((), ())), preferred_element_type=f32
            )
            work[k, 0:128, :width] = work[k, 0:128, :width] - change
        third = [load(k, below) for k in every]
        fourth = [load(k, pl.multiple_of(below + 8, 8)) for k in every]
        first_done = lockstep(eliminate(panels[k][0], shift_a) for k in every)
        second = lockstep(update(panels[k][1], shift_a, first_done[k]) for k in every)
        mixed = lockstep(
            [eliminate(second[k], shift_b) for k in every]
            + [update(third[k], shift_a, first_done[k]) for k in every]
            + [update(fourth[k], shift_a, first_done[k]) for k in every]
        )
        second_done = mixed[:count]
        later = lockstep(
            update(mixed[count + i], shift_b, second_done[i % count]) for i in range(2 * count)
        )
        rows = []
        for k in every:
            pair = [jnp.concatenate(part[k][3], 1) for part in (first_done, second_done)]
            pair = jnp.concatenate(pair, 0)
            upper[k, pl.ds(here, 16), : 128 * widths[k]] = pair
            rows.append(pair)
        return rows, [(later[k], later[count + k]) for k in every]

    start = (
        [jnp.zeros((16, 128 * widths[k]), f32) for k in every],
        [(load(k, 0), load(k, 8)) for k in every],
    )
    lax.fori_loop(0, RANK // 16, pair_step, start)


def reduce_all(grams, refs):
    work, upper, last = refs
    count = len(grams)
    unit = identity()
    images = []
    for k, (g00, g01, g11) in enumerate(grams):
        stacked = whole_gram(g00, g01, g01.T, g11)
        image = (stacked[:, 0:128] + stacked[:, 128:256]) * ROOT_HALF
        images.append(image)
        products = tn(image, jnp.concatenate([image, nn(stacked, image)], 1))
        work[k, 0:128, 0:128] = products[:, 0:128]
        work[k, 0:128, 128:256] = unit
        work[count + k, 0:128, 0:128] = products[:, 128:256]
    factor(work, upper, last, [2] * count + [1] * count)
    rows = lax.broadcasted_iota(jnp.int32, (RANK, RANK), 0)
    lanes = lax.broadcasted_iota(jnp.int32, (RANK, RANK), 1)
    roots, inners, spans = [], [], []
    for k, (g00, g01, g11) in enumerate(grams):
        inverse = upper[k, :, 128:256]
        turned = jnp.where(lanes >= rows, upper[count + k, :, 0:128], 0.0)
        root = nt(turned, inverse)
        inner = nt(root, root)
        tail = (trace(g00) + trace(g11) - trace(inner)) / RANK
        work[k, 0:128, 0:128] = inner + tail * unit
        work[k, 0:128, 128:256] = unit
        roots.append(root)
        inners.append(inner)
        spans.append(nt(inverse, images[k]))
    factor(work, upper, last, [2] * count)
    outs = []
    for k in range(count):
        inverse = upper[k, :, 128:256]
        both = nn(inverse, jnp.concatenate([roots[k], inners[k]], 1))
        square = both[:, 128:256]
        outs.append((nn(both[:, 0:128], spans[k]), nt(square, square)))
    return outs


def whole_gram(g00, g01, g10, g11):
    return jnp.concatenate(
        [jnp.concatenate([g00, g01], 1), jnp.concatenate([g10, g11], 1)], 0
    )


def scratch(count):
    return [
        pltpu.VMEM((2 * count, RANK + 16, 256), f32),
        pltpu.VMEM((2 * count, RANK, 256), f32),
        pltpu.VMEM((2 * count, 8, 256), f32),
    ]


def on_core(kernel, outs, scratches, *operands):
    vmem = pl.BlockSpec(memory_space=pltpu.VMEM)
    return pl.pallas_call(
        kernel,
        out_shape=[jax.ShapeDtypeStruct(shape, dtype) for shape, dtype in outs],
        in_specs=[vmem] * len(operands),
        out_specs=[vmem] * len(outs),
        scratch_shapes=scratches,
        compiler_params=pltpu.CompilerParams(vmem_limit_bytes=40 << 20),
    )(*operands)


SLAB = ((0, 0), (0, 1), (1, 1), (2, 2), (2, 3), (3, 3), (0, 2), (0, 3), (1, 2), (1, 3))


def slab_gram_kernel(own, other, out):
    rows = jnp.concatenate([own[...], other[...].astype(bf16)], 0)
    gram = lax.dot_general(rows, rows, (((1,), (1,)), ((), ())), preferred_element_type=f32)
    for place, (a, b) in enumerate(SLAB):
        out[128 * place : 128 * place + 128] = gram[
            128 * a : 128 * a + 128, 128 * b : 128 * b + 128
        ]


def blocks_of(gram, pairs):
    return {pair: gram[128 * n : 128 * n + 128] for n, pair in enumerate(pairs)}


def slab_kernel(
    facts, gram, own, other, block, prefix, block_gram, prefix_gram, work, upper, last
):
    refs = (work, upper, last)
    g = blocks_of(gram, SLAB)
    (mine, my_gram), (theirs, their_gram) = reduce_all(
        [(g[0, 0], g[0, 1], g[1, 1]), (g[2, 2], g[2, 3], g[3, 3])], refs
    )
    across = nt(nn(mine, whole_gram(g[0, 2], g[0, 3], g[1, 2], g[1, 3])), theirs)
    ((mixing, merged_gram),) = reduce_all([(my_gram, across, their_gram)], refs)
    own_sketch = nn(mine, own[...].astype(f32))
    other_sketch = nn(theirs, other[...])
    merged = nn(mixing, jnp.concatenate([own_sketch, other_sketch], 0))
    take = facts[0:1, 0:1] > 0.5
    block[...] = merged
    block_gram[...] = merged_gram
    prefix[...] = jnp.where(take, merged, own_sketch)
    prefix_gram[...] = jnp.where(take, merged_gram, my_gram)


def whole(core, kept, swapped):
    top = jnp.where(core, swapped, kept)
    low = jnp.where(core, kept, swapped)
    return jnp.concatenate([top, low], 0)


OUTER = ((1, 1), (1, 2), (1, 3), (1, 4), (2, 2), (2, 3), (2, 4), (3, 3), (3, 4))
INNER = OUTER + ((0, 1), (0, 2), (0, 3))


def gram_kernel(with_rows, facts, kept, swapped, block, prefix, *rest):
    rows, (grams, peers) = (rest[0], rest[1:]) if with_rows else (None, rest)
    core = facts[2:3, 0:1] > 0.5
    sketches = [block[...]]
    for j in range(3):
        sketches.append(whole(core, kept[j], swapped[j]))
        peers[j] = sketches[-1]
    sketches.append(prefix[...])

    def put(place, left, right):
        product = nt(left, jnp.concatenate(right, 0))
        size = left.shape[0]
        for n in range(len(right)):
            grams[place : place + size] = product[:, 128 * n : 128 * n + 128]
            place += size
        return place

    place = put(0, sketches[1], sketches[1:5])
    place = put(place, sketches[2], sketches[2:5])
    place = put(place, sketches[3], sketches[3:5])
    if with_rows:
        put(place, rows[...].astype(f32), [sketches[a] for a in (2, 3, 1, 4)])
    else:
        put(place, sketches[0], sketches[1:4])


def merge_prefix(take_near, g, far, near, near_gram, prefix_gram):
    unit = identity()
    mixing = jnp.where(take_near, near, jnp.concatenate([jnp.zeros_like(unit), unit], 1))
    gram = jnp.where(take_near, near_gram, prefix_gram)
    with_rows = nn(far, whole_gram(g[1, 2].T, g[2, 4], g[1, 3].T, g[3, 4]))
    return mixing, gram, nt(with_rows, mixing)


def combine_prefix(take_far, far, near, merged):
    first = jnp.where(take_far, nn(merged[:, 0:128], far), 0.0)
    second = jnp.where(take_far, nn(merged[:, 128:256], near), near)
    return jnp.concatenate([first, second], 1)


def inner_kernel(
    facts, gram, block, peers, prefix, block_gram, prefix_gram,
    new_block, new_prefix, new_prefix_gram, work, upper, last,
):
    refs = (work, upper, last)
    g = blocks_of(gram, INNER)
    take_near, take_far = facts[0:1, 0:1] > 0.5, facts[1:2, 0:1] > 0.5
    (pair, pair_gram), (far, far_gram), (near, near_gram) = reduce_all(
        [
            (block_gram[...], g[0, 1], g[1, 1]),
            (g[2, 2], g[2, 3], g[3, 3]),
            (g[1, 1], g[1, 4], prefix_gram[...]),
        ],
        refs,
    )
    across_blocks = nt(nn(pair, whole_gram(g[0, 2], g[0, 3], g[1, 2], g[1, 3])), far)
    near, near_gram, across = merge_prefix(
        take_near, g, far, near, near_gram, prefix_gram[...]
    )
    (merged_block, _), (merged, merged_gram) = reduce_all(
        [(pair_gram, across_blocks, far_gram), (far_gram, across, near_gram)], refs
    )
    own_pair = jnp.concatenate([block[...], peers[0]], 0)
    far_pair = jnp.concatenate([peers[1], peers[2]], 0)
    halves = jnp.concatenate([nn(pair, own_pair), nn(far, far_pair)], 0)
    new_block[...] = nn(merged_block, halves)
    coefs = combine_prefix(take_far, far, near, merged)
    new_prefix[...] = nn(coefs, jnp.concatenate([far_pair, peers[0], prefix[...]], 0))
    new_prefix_gram[...] = jnp.where(take_far, merged_gram, near_gram)


def outer_kernel(facts, gram, peers, prefix, prefix_gram, rows, out, work, upper, last):
    refs = (work, upper, last)
    g = blocks_of(gram, OUTER)
    take_near, take_far = facts[0:1, 0:1] > 0.5, facts[1:2, 0:1] > 0.5
    (far, far_gram), (near, near_gram) = reduce_all(
        [
            (g[2, 2], g[2, 3], g[3, 3]),
            (g[1, 1], g[1, 4], prefix_gram[...]),
        ],
        refs,
    )
    near, near_gram, across = merge_prefix(
        take_near, g, far, near, near_gram, prefix_gram[...]
    )
    ((merged, merged_gram),) = reduce_all([(far_gram, across, near_gram)], refs)
    scale = facts[3:4, 0:1]
    coefs = combine_prefix(take_far, far, near, merged) * scale
    scaled = nn(coefs, jnp.concatenate([peers[1], peers[2], peers[0], prefix[...]], 0))
    half_basis = scaled.astype(bf16)
    start = 128 * len(OUTER)
    projection = nt(
        jnp.concatenate([gram[start + 256 * n : start + 256 * n + 256] for n in range(4)], 1),
        coefs,
    )
    unit = identity()
    shifted = unit + jnp.where(take_far, merged_gram, near_gram) * (scale * scale)
    size = jnp.sqrt(jnp.sum(shifted * shifted, keepdims=True))
    current = shifted / size
    partner = unit
    for repeat in range(ROOT_STEPS):
        middle = 1.5 * unit - 0.5 * (nn(partner, current) if repeat else current)
        current = nn(current, middle)
        if repeat + 1 < ROOT_STEPS:
            partner = nn(middle, partner) if repeat else middle
    total = shifted + current * jnp.sqrt(size)
    total = 0.5 * (total + total.T)
    work[0, 0:128, 0:128] = total
    work[0, 0:128, 128:256] = unit
    factor(work, upper, last, [2])
    inverse = upper[0, :, 128:256]
    coefficients = nn(nt(projection, inverse), inverse)
    restored = jnp.dot(coefficients.astype(bf16), half_basis, preferred_element_type=f32)
    out[...] = ((rows[...].astype(f32) - restored) * facts[4:5, 0:1]).astype(bf16)


def over_features(partial):
    count = lax.axis_size("feat")
    share, width = partial.shape[0] // count, partial.shape[1]
    pieces = lax.all_to_all(
        partial.reshape(count, share, width), "feat", split_axis=0, concat_axis=0, tiled=True
    )
    total = jnp.sum(pieces, axis=0)
    copies = jnp.broadcast_to(total, (count, share, width))
    everything = lax.all_to_all(copies, "feat", split_axis=0, concat_axis=0, tiled=True)
    return everything.reshape(count * share, width)


def from_partner(block, flips, wanted=None):
    route = [
        (s, s ^ flips)
        for s in range(lax.axis_size("seq"))
        if wanted is None or (s ^ flips) & wanted == wanted
    ]
    return lax.ppermute(block, "seq", route)


def peers_of(block, near, far, core, one_way):
    half = lax.dynamic_slice_in_dim(block, core * HALF, HALF, 0)
    kept = jnp.stack(
        [
            from_partner(half, near, near if one_way else None),
            from_partner(half, far, far if one_way else None),
            from_partner(half, near | far, far if one_way else None),
        ]
    )
    return kept, from_partner(kept, 1)


def on_device(activations, ridge_scale):
    seq_index = lax.axis_index("seq")
    width = activations.shape[1]
    core = seq_index % 2
    seen_rows = ((seq_index + 1) * activations.shape[0]).astype(f32)

    def facts_of(near, far):
        values = [
            (seq_index // near % 2).astype(f32),
            (seq_index // far % 2).astype(f32),
            core.astype(f32),
            lax.rsqrt(seen_rows * ridge_scale),
            lax.rsqrt(ridge_scale),
        ]
        values += [jnp.zeros((), f32)] * 3
        return jnp.broadcast_to(jnp.stack(values)[:, None], (8, 128))

    other = from_partner(activations.astype(f32), 1)
    (partial,) = on_core(
        slab_gram_kernel, [((128 * len(SLAB), 128), f32)], [], activations, other
    )
    gram = over_features(partial)
    sketch, square = ((RANK, width), f32), ((RANK, RANK), f32)
    block, prefix, block_gram, prefix_gram = on_core(
        slab_kernel,
        [sketch, sketch, square, square],
        scratch(2),
        facts_of(1, 1), gram, activations, other,
    )

    facts = facts_of(2, 4)
    kept, swapped = peers_of(block, 2, 4, core, False)
    partial, peers = on_core(
        functools.partial(gram_kernel, False),
        [((128 * len(INNER), 128), f32), ((3, RANK, width), f32)],
        [],
        facts, kept, swapped, block, prefix,
    )
    gram = over_features(partial)
    block, prefix, prefix_gram = on_core(
        inner_kernel,
        [sketch, sketch, square],
        scratch(3),
        facts, gram, block, peers, prefix, block_gram, prefix_gram,
    )

    facts = facts_of(8, 16)
    kept, swapped = peers_of(block, 8, 16, core, True)
    partial, peers = on_core(
        functools.partial(gram_kernel, True),
        [((128 * (len(OUTER) + 8), 128), f32), ((3, RANK, width), f32)],
        [],
        facts, kept, swapped, block, prefix, activations,
    )
    gram = over_features(partial)
    (whitened,) = on_core(
        outer_kernel,
        [(activations.shape, bf16)],
        scratch(2),
        facts, gram, peers, prefix, prefix_gram, activations,
    )
    return whitened


def solution(mesh):
    placed = (P("seq", "feat"), P())
    return jax.shard_map(
        on_device, mesh=mesh, in_specs=placed, out_specs=P("seq", "feat"), check_vma=False
    )
```

```python
import functools

import jax
import jax.numpy as jnp
from jax import lax
from jax.experimental import pallas as pl
from jax.experimental.pallas import tpu as pltpu
from jax.sharding import PartitionSpec as P

RANK = 128
ROOT_STEPS = 12
HALF = RANK // 2

f32 = jnp.float32
bf16 = jnp.bfloat16
precise = lax.Precision.HIGHEST
ROOT_HALF = 0.7071067811865476


def nn(a, b):
    return lax.dot_general(
        a, b, (((1,), (0,)), ((), ())), precision=precise, preferred_element_type=f32
    )


def nt(a, b):
    return lax.dot_general(
        a, b, (((1,), (1,)), ((), ())), precision=precise, preferred_element_type=f32
    )


def tn(a, b):
    return lax.dot_general(
        a, b, (((0,), (0,)), ((), ())), precision=precise, preferred_element_type=f32
    )


def eye_mask():
    rows = lax.broadcasted_iota(jnp.int32, (RANK, RANK), 0)
    lanes = lax.broadcasted_iota(jnp.int32, (RANK, RANK), 1)
    return rows == lanes


def identity():
    return jnp.where(eye_mask(), 1.0, 0.0).astype(f32)


def trace(matrix):
    return jnp.sum(jnp.where(eye_mask(), matrix, 0.0), keepdims=True)


def parts_of(rows):
    high = rows.astype(bf16).astype(f32)
    rest = rows - high
    middle = rest.astype(bf16).astype(f32)
    return high, middle, rest - middle


def factor(work, upper, last, widths):
    if len(widths) == 1:
        return factor_by_pairs(work, upper, widths)
    tile = (8, 128)
    sub = lax.broadcasted_iota(jnp.int32, tile, 0)
    lane = lax.broadcasted_iota(jnp.int32, tile, 1)
    count = len(widths)
    for k in range(count):
        last[k] = jnp.zeros_like(last[k])

    def cols(c):
        return slice(128 * c, 128 * c + 128)

    def panel_step(step, carry):
        here = pl.multiple_of(8 * step, 8)
        below = pl.multiple_of(8 * step + 8, 8)
        shift = lax.rem(128 - here, 128)
        panels = [
            [work[k, pl.ds(here, 8), cols(c)] for c in range(widths[k])] for k in range(count)
        ]
        for k in range(count):
            width = 128 * widths[k]
            high, middle, low = parts_of(last[k][:, :width])
            keep = lane >= below
            lh, lm, ll = [jnp.where(keep, part[:, :128], 0.0) for part in (high, middle, low)]
            left = jnp.concatenate([lh, lh, lm, lh, ll, lm], 0).astype(bf16)
            right = jnp.concatenate([high, middle, high, low, high, middle], 0).astype(bf16)
            update = lax.dot_general(
                left, right, (((0,), (0,)), ((), ())), preferred_element_type=f32
            )
            work[k, 0:128, :width] = work[k, 0:128, :width] - update
        for k in range(count):
            block = pltpu.roll(panels[k][0], shift, 1)
            splat = {
                (i, c): jnp.broadcast_to(block[i : i + 1, c : c + 1], tile)
                for i in range(8)
                for c in range(i, 8)
            }
            rows = [
                [jnp.broadcast_to(piece[i : i + 1, :], tile) for i in range(8)]
                for piece in panels[k]
            ]
            scales = []
            for r in range(8):
                scale = lax.rsqrt(splat[r, r])
                scales.append(scale)
                for c in range(r, 8):
                    splat[r, c] = splat[r, c] * scale
                for piece in rows:
                    piece[r] = piece[r] * scale
                for i in range(r + 1, 8):
                    multiplier = splat[r, i]
                    for c in range(i, 8):
                        splat[i, c] = splat[i, c] - multiplier * splat[r, c]
                    for piece in rows:
                        piece[i] = piece[i] - multiplier * piece[r]
            for c, piece in enumerate(rows):
                done = piece[0]
                for r in range(1, 8):
                    done = jnp.where(sub == r, piece[r], done)
                upper[k, pl.ds(here, 8), cols(c)] = done
                last[k, :, cols(c)] = done
            following = [work[k, pl.ds(below, 8), cols(c)] for c in range(widths[k])]
            block = pltpu.roll(following[0], shift, 1)
            heads = [jnp.broadcast_to(block[:, c : c + 1], tile) for c in range(8)]
            for r in range(8):
                multiplier = heads[r] * scales[r]
                for c in range(r + 1, 8):
                    heads[c] = heads[c] - multiplier * splat[r, c]
                for c in range(widths[k]):
                    following[c] = following[c] - multiplier * rows[c][r]
            for c in range(widths[k]):
                work[k, pl.ds(below, 8), cols(c)] = following[c]
        return carry

    lax.fori_loop(0, RANK // 8, panel_step, 0)


def lockstep(steps):
    steps, results = list(steps), {}
    live = list(range(len(steps)))
    while live:
        for i in list(live):
            try:
                next(steps[i])
            except StopIteration as stop:
                results[i] = stop.value
                live.remove(i)
    return [results[i] for i in range(len(steps))]


def eliminate(pieces, shift):
    tile = (8, 128)
    sub = lax.broadcasted_iota(jnp.int32, tile, 0)
    block = pltpu.roll(pieces[0], shift, 1)
    splat = {
        (i, c): jnp.broadcast_to(block[i : i + 1, c : c + 1], tile)
        for i in range(8)
        for c in range(i, 8)
    }
    rows = [[jnp.broadcast_to(piece[i : i + 1, :], tile) for i in range(8)] for piece in pieces]
    scales = []
    yield
    for r in range(8):
        scale = lax.rsqrt(splat[r, r])
        scales.append(scale)
        for c in range(r, 8):
            splat[r, c] = splat[r, c] * scale
        for piece in rows:
            piece[r] = piece[r] * scale
        for i in range(r + 1, 8):
            multiplier = splat[r, i]
            for c in range(i, 8):
                splat[i, c] = splat[i, c] - multiplier * splat[r, c]
            for piece in rows:
                piece[i] = piece[i] - multiplier * piece[r]
        yield
    done = []
    for piece in rows:
        merged = piece[0]
        for r in range(1, 8):
            merged = jnp.where(sub == r, piece[r], merged)
        done.append(merged)
    return splat, rows, scales, done


def update(pieces, shift, factored):
    splat, rows, scales, _ = factored
    block = pltpu.roll(pieces[0], shift, 1)
    heads = [jnp.broadcast_to(block[:, c : c + 1], (8, 128)) for c in range(8)]
    pieces = list(pieces)
    yield
    for r in range(8):
        multiplier = heads[r] * scales[r]
        for c in range(r + 1, 8):
            heads[c] = heads[c] - multiplier * splat[r, c]
        for c in range(len(pieces)):
            pieces[c] = pieces[c] - multiplier * rows[c][r]
        yield
    return pieces


def factor_by_pairs(work, upper, widths):
    count = len(widths)
    every = range(count)
    lane = lax.broadcasted_iota(jnp.int32, (16, 128), 1)

    def load(k, start):
        return [work[k, pl.ds(start, 8), 128 * c : 128 * c + 128] for c in range(widths[k])]

    def pair_step(step, carry):
        before, panels = carry
        here = pl.multiple_of(16 * step, 16)
        below = pl.multiple_of(16 * step + 16, 16)
        shift_a, shift_b = lax.rem(128 - here, 128), lax.rem(248 - here, 128)
        for k in every:
            width = 128 * widths[k]
            high, middle, low = parts_of(before[k])
            keep = lane >= below
            lh, lm, ll = [jnp.where(keep, part[:, :128], 0.0) for part in (high, middle, low)]
            left = jnp.concatenate([lh, lh, lm, lh, ll, lm], 0).astype(bf16)
            right = jnp.concatenate([high, middle, high, low, high, middle], 0).astype(bf16)
            change = lax.dot_general(
                left, right, (((0,), (0,)), ((), ())), preferred_element_type=f32
            )
            work[k, 0:128, :width] = work[k, 0:128, :width] - change
        third = [load(k, below) for k in every]
        fourth = [load(k, pl.multiple_of(below + 8, 8)) for k in every]
        first_done = lockstep(eliminate(panels[k][0], shift_a) for k in every)
        second = lockstep(update(panels[k][1], shift_a, first_done[k]) for k in every)
        mixed = lockstep(
            [eliminate(second[k], shift_b) for k in every]
            + [update(third[k], shift_a, first_done[k]) for k in every]
            + [update(fourth[k], shift_a, first_done[k]) for k in every]
        )
        second_done = mixed[:count]
        later = lockstep(
            update(mixed[count + i], shift_b, second_done[i % count]) for i in range(2 * count)
        )
        rows = []
        for k in every:
            pair = [jnp.concatenate(part[k][3], 1) for part in (first_done, second_done)]
            pair = jnp.concatenate(pair, 0)
            upper[k, pl.ds(here, 16), : 128 * widths[k]] = pair
            rows.append(pair)
        return rows, [(later[k], later[count + k]) for k in every]

    start = (
        [jnp.zeros((16, 128 * widths[k]), f32) for k in every],
        [(load(k, 0), load(k, 8)) for k in every],
    )
    lax.fori_loop(0, RANK // 16, pair_step, start)


def reduce_all(grams, refs):
    work, upper, last = refs
    count = len(grams)
    unit = identity()
    images = []
    for k, (g00, g01, g11) in enumerate(grams):
        stacked = whole_gram(g00, g01, g01.T, g11)
        image = (stacked[:, 0:128] + stacked[:, 128:256]) * ROOT_HALF
        images.append(image)
        products = tn(image, jnp.concatenate([image, nn(stacked, image)], 1))
        work[k, 0:128, 0:128] = products[:, 0:128]
        work[k, 0:128, 128:256] = unit
        work[count + k, 0:128, 0:128] = products[:, 128:256]
    factor(work, upper, last, [2] * count + [1] * count)
    rows = lax.broadcasted_iota(jnp.int32, (RANK, RANK), 0)
    lanes = lax.broadcasted_iota(jnp.int32, (RANK, RANK), 1)
    roots, inners, spans = [], [], []
    for k, (g00, g01, g11) in enumerate(grams):
        inverse = upper[k, :, 128:256]
        turned = jnp.where(lanes >= rows, upper[count + k, :, 0:128], 0.0)
        root = nt(turned, inverse)
        inner = nt(root, root)
        tail = (trace(g00) + trace(g11) - trace(inner)) / RANK
        work[k, 0:128, 0:128] = inner + tail * unit
        work[k, 0:128, 128:256] = unit
        roots.append(root)
        inners.append(inner)
        spans.append(nt(inverse, images[k]))
    factor(work, upper, last, [2] * count)
    outs = []
    for k in range(count):
        inverse = upper[k, :, 128:256]
        both = nn(inverse, jnp.concatenate([roots[k], inners[k]], 1))
        square = both[:, 128:256]
        outs.append((nn(both[:, 0:128], spans[k]), nt(square, square)))
    return outs


def whole_gram(g00, g01, g10, g11):
    return jnp.concatenate(
        [jnp.concatenate([g00, g01], 1), jnp.concatenate([g10, g11], 1)], 0
    )


def scratch(count):
    return [
        pltpu.VMEM((2 * count, RANK + 16, 256), f32),
        pltpu.VMEM((2 * count, RANK, 256), f32),
        pltpu.VMEM((2 * count, 8, 256), f32),
    ]


def on_core(kernel, outs, scratches, *operands):
    vmem = pl.BlockSpec(memory_space=pltpu.VMEM)
    return pl.pallas_call(
        kernel,
        out_shape=[jax.ShapeDtypeStruct(shape, dtype) for shape, dtype in outs],
        in_specs=[vmem] * len(operands),
        out_specs=[vmem] * len(outs),
        scratch_shapes=scratches,
        compiler_params=pltpu.CompilerParams(vmem_limit_bytes=40 << 20),
    )(*operands)


SLAB = ((0, 0), (0, 1), (1, 1), (2, 2), (2, 3), (3, 3), (0, 2), (0, 3), (1, 2), (1, 3))


def slab_gram_kernel(own, other, out):
    rows = jnp.concatenate([own[...], other[...].astype(bf16)], 0)
    gram = lax.dot_general(rows, rows, (((1,), (1,)), ((), ())), preferred_element_type=f32)
    for place, (a, b) in enumerate(SLAB):
        out[128 * place : 128 * place + 128] = gram[
            128 * a : 128 * a + 128, 128 * b : 128 * b + 128
        ]


def blocks_of(gram, pairs):
    return {pair: gram[128 * n : 128 * n + 128] for n, pair in enumerate(pairs)}


def slab_kernel(
    facts, gram, own, other, block, prefix, block_gram, prefix_gram, work, upper, last
):
    refs = (work, upper, last)
    g = blocks_of(gram, SLAB)
    (mine, my_gram), (theirs, their_gram) = reduce_all(
        [(g[0, 0], g[0, 1], g[1, 1]), (g[2, 2], g[2, 3], g[3, 3])], refs
    )
    across = nt(nn(mine, whole_gram(g[0, 2], g[0, 3], g[1, 2], g[1, 3])), theirs)
    ((mixing, merged_gram),) = reduce_all([(my_gram, across, their_gram)], refs)
    own_sketch = nn(mine, own[...].astype(f32))
    other_sketch = nn(theirs, other[...])
    merged = nn(mixing, jnp.concatenate([own_sketch, other_sketch], 0))
    take = facts[0:1, 0:1] > 0.5
    block[...] = merged
    block_gram[...] = merged_gram
    prefix[...] = jnp.where(take, merged, own_sketch)
    prefix_gram[...] = jnp.where(take, merged_gram, my_gram)


def whole(core, kept, swapped):
    top = jnp.where(core, swapped, kept)
    low = jnp.where(core, kept, swapped)
    return jnp.concatenate([top, low], 0)


OUTER = ((1, 1), (1, 2), (1, 3), (1, 4), (2, 2), (2, 3), (2, 4), (3, 3), (3, 4))
INNER = OUTER + ((0, 1), (0, 2), (0, 3))


def gram_kernel(with_rows, facts, kept, swapped, block, prefix, *rest):
    rows, (grams, peers) = (rest[0], rest[1:]) if with_rows else (None, rest)
    core = facts[2:3, 0:1] > 0.5
    sketches = [block[...]]
    for j in range(3):
        sketches.append(whole(core, kept[j], swapped[j]))
        peers[j] = sketches[-1]
    sketches.append(prefix[...])

    def put(place, left, right):
        product = nt(left, jnp.concatenate(right, 0))
        size = left.shape[0]
        for n in range(len(right)):
            grams[place : place + size] = product[:, 128 * n : 128 * n + 128]
            place += size
        return place

    place = put(0, sketches[1], sketches[1:5])
    place = put(place, sketches[2], sketches[2:5])
    place = put(place, sketches[3], sketches[3:5])
    if with_rows:
        put(place, rows[...].astype(f32), [sketches[a] for a in (2, 3, 1, 4)])
    else:
        put(place, sketches[0], sketches[1:4])


def merge_prefix(take_near, g, far, near, near_gram, prefix_gram):
    unit = identity()
    mixing = jnp.where(take_near, near, jnp.concatenate([jnp.zeros_like(unit), unit], 1))
    gram = jnp.where(take_near, near_gram, prefix_gram)
    with_rows = nn(far, whole_gram(g[1, 2].T, g[2, 4], g[1, 3].T, g[3, 4]))
    return mixing, gram, nt(with_rows, mixing)


def combine_prefix(take_far, far, near, merged):
    first = jnp.where(take_far, nn(merged[:, 0:128], far), 0.0)
    second = jnp.where(take_far, nn(merged[:, 128:256], near), near)
    return jnp.concatenate([first, second], 1)


def inner_kernel(
    facts, gram, block, peers, prefix, block_gram, prefix_gram,
    new_block, new_prefix, new_prefix_gram, work, upper, last,
):
    refs = (work, upper, last)
    g = blocks_of(gram, INNER)
    take_near, take_far = facts[0:1, 0:1] > 0.5, facts[1:2, 0:1] > 0.5
    (pair, pair_gram), (far, far_gram), (near, near_gram) = reduce_all(
        [
            (block_gram[...], g[0, 1], g[1, 1]),
            (g[2, 2], g[2, 3], g[3, 3]),
            (g[1, 1], g[1, 4], prefix_gram[...]),
        ],
        refs,
    )
    across_blocks = nt(nn(pair, whole_gram(g[0, 2], g[0, 3], g[1, 2], g[1, 3])), far)
    near, near_gram, across = merge_prefix(
        take_near, g, far, near, near_gram, prefix_gram[...]
    )
    (merged_block, _), (merged, merged_gram) = reduce_all(
        [(pair_gram, across_blocks, far_gram), (far_gram, across, near_gram)], refs
    )
    own_pair = jnp.concatenate([block[...], peers[0]], 0)
    far_pair = jnp.concatenate([peers[1], peers[2]], 0)
    halves = jnp.concatenate([nn(pair, own_pair), nn(far, far_pair)], 0)
    new_block[...] = nn(merged_block, halves)
    coefs = combine_prefix(take_far, far, near, merged)
    new_prefix[...] = nn(coefs, jnp.concatenate([far_pair, peers[0], prefix[...]], 0))
    new_prefix_gram[...] = jnp.where(take_far, merged_gram, near_gram)


def outer_kernel(facts, gram, peers, prefix, prefix_gram, rows, out, work, upper, last):
    refs = (work, upper, last)
    g = blocks_of(gram, OUTER)
    take_near, take_far = facts[0:1, 0:1] > 0.5, facts[1:2, 0:1] > 0.5
    (far, far_gram), (near, near_gram) = reduce_all(
        [
            (g[2, 2], g[2, 3], g[3, 3]),
            (g[1, 1], g[1, 4], prefix_gram[...]),
        ],
        refs,
    )
    near, near_gram, across = merge_prefix(
        take_near, g, far, near, near_gram, prefix_gram[...]
    )
    ((merged, merged_gram),) = reduce_all([(far_gram, across, near_gram)], refs)
    scale = facts[3:4, 0:1]
    coefs = combine_prefix(take_far, far, near, merged) * scale
    scaled = nn(coefs, jnp.concatenate([peers[1], peers[2], peers[0], prefix[...]], 0))
    half_basis = scaled.astype(bf16)
    start = 128 * len(OUTER)
    projection = nt(
        jnp.concatenate([gram[start + 256 * n : start + 256 * n + 256] for n in range(4)], 1),
        coefs,
    )
    unit = identity()
    shifted = unit + jnp.where(take_far, merged_gram, near_gram) * (scale * scale)
    size = jnp.sqrt(jnp.sum(shifted * shifted, keepdims=True))
    work[1, 0:128, 0:128] = shifted / size
    work[1, 0:128, 128:256] = unit

    def root_step(repeat, carry):
        current, partner = work[1, 0:128, 0:128], work[1, 0:128, 128:256]
        middle = 1.5 * unit - 0.5 * nn(partner, current)
        work[1, 0:128, 0:128] = nn(current, middle)
        work[1, 0:128, 128:256] = nn(middle, partner)
        return carry

    lax.fori_loop(0, ROOT_STEPS, root_step, 0)
    current = work[1, 0:128, 0:128]
    total = shifted + current * jnp.sqrt(size)
    total = 0.5 * (total + total.T)
    work[0, 0:128, 0:128] = total
    work[0, 0:128, 128:256] = unit
    factor(work, upper, last, [2])
    inverse = upper[0, :, 128:256]
    coefficients = nn(nt(projection, inverse), inverse)
    restored = jnp.dot(coefficients.astype(bf16), half_basis, preferred_element_type=f32)
    out[...] = ((rows[...].astype(f32) - restored) * facts[4:5, 0:1]).astype(bf16)


def over_features(partial):
    count = lax.axis_size("feat")
    share, width = partial.shape[0] // count, partial.shape[1]
    pieces = lax.all_to_all(
        partial.reshape(count, share, width), "feat", split_axis=0, concat_axis=0, tiled=True
    )
    total = jnp.sum(pieces, axis=0)
    copies = jnp.broadcast_to(total, (count, share, width))
    everything = lax.all_to_all(copies, "feat", split_axis=0, concat_axis=0, tiled=True)
    return everything.reshape(count * share, width)


def from_partner(block, flips, wanted=None):
    route = [
        (s, s ^ flips)
        for s in range(lax.axis_size("seq"))
        if wanted is None or (s ^ flips) & wanted == wanted
    ]
    return lax.ppermute(block, "seq", route)


def peers_of(block, near, far, core, one_way):
    half = lax.dynamic_slice_in_dim(block, core * HALF, HALF, 0)
    kept = jnp.stack(
        [
            from_partner(half, near, near if one_way else None),
            from_partner(half, far, far if one_way else None),
            from_partner(half, near | far, far if one_way else None),
        ]
    )
    return kept, from_partner(kept, 1)


def on_device(activations, ridge_scale):
    seq_index = lax.axis_index("seq")
    width = activations.shape[1]
    core = seq_index % 2
    seen_rows = ((seq_index + 1) * activations.shape[0]).astype(f32)

    def facts_of(near, far):
        values = [
            (seq_index // near % 2).astype(f32),
            (seq_index // far % 2).astype(f32),
            core.astype(f32),
            lax.rsqrt(seen_rows * ridge_scale),
            lax.rsqrt(ridge_scale),
        ]
        values += [jnp.zeros((), f32)] * 3
        return jnp.broadcast_to(jnp.stack(values)[:, None], (8, 128))

    other = from_partner(activations.astype(f32), 1)
    (partial,) = on_core(
        slab_gram_kernel, [((128 * len(SLAB), 128), f32)], [], activations, other
    )
    gram = over_features(partial)
    sketch, square = ((RANK, width), f32), ((RANK, RANK), f32)
    block, prefix, block_gram, prefix_gram = on_core(
        slab_kernel,
        [sketch, sketch, square, square],
        scratch(2),
        facts_of(1, 1), gram, activations, other,
    )

    facts = facts_of(2, 4)
    kept, swapped = peers_of(block, 2, 4, core, False)
    partial, peers = on_core(
        functools.partial(gram_kernel, False),
        [((128 * len(INNER), 128), f32), ((3, RANK, width), f32)],
        [],
        facts, kept, swapped, block, prefix,
    )
    gram = over_features(partial)
    block, prefix, prefix_gram = on_core(
        inner_kernel,
        [sketch, sketch, square],
        scratch(3),
        facts, gram, block, peers, prefix, block_gram, prefix_gram,
    )

    facts = facts_of(8, 16)
    kept, swapped = peers_of(block, 8, 16, core, True)
    partial, peers = on_core(
        functools.partial(gram_kernel, True),
        [((128 * (len(OUTER) + 8), 128), f32), ((3, RANK, width), f32)],
        [],
        facts, kept, swapped, block, prefix, activations,
    )
    gram = over_features(partial)
    (whitened,) = on_core(
        outer_kernel,
        [(activations.shape, bf16)],
        scratch(2),
        facts, gram, peers, prefix, prefix_gram, activations,
    )
    return whitened


def solution(mesh):
    placed = (P("seq", "feat"), P())
    return jax.shard_map(
        on_device, mesh=mesh, in_specs=placed, out_specs=P("seq", "feat"), check_vma=False
    )
```
